32 devices in a mesh: group: 8 (over y, x, core), tensor: 4 (over z).
Axes of the slice: x: 2, y: 2, z: 4, core: 2. Of those that a mesh axis runs over, the one named last changes fastest.
Arguments:
- hidden: bfloat16 [8, 2, 256, 4096], P('group', None, 'tensor'), may hold values from -6 to 6
- norm_gain: bfloat16 [4096], replicated, may hold values from 0.5 to 1.5
- w_query: bfloat16 [4096, 4096], P(None, 'tensor'), may hold values from -0.09375 to 0.09375
- w_key: bfloat16 [4096, 1024], P(None, 'tensor'), may hold values from -0.09375 to 0.09375
- w_value: bfloat16 [4096, 1024], P(None, 'tensor'), may hold values from -0.09375 to 0.09375
- w_output: bfloat16 [4096, 4096], P('tensor'), may hold values from -0.09375 to 0.09375
- prefix_pool: bfloat16 [16384, 8, 2048], P('group', None, 'tensor'), may hold values from -120 to 120
- page_table: int32 [8, 2, 1024], P('group'), may hold values from 0 to 1023, each once within a row
- prefix_len: int32 [8, 2], replicated, may hold values from 1024 to 8192
- source: int32 [8], replicated, may hold values from 0 to 7, as said below
- decode_owner: int32 [8, 32], replicated, may hold values from 0 to 7, as said below
Outputs:
- layer_out: bfloat16 [2048, 4096], P(('group', 'tensor'))
- decode_pool: bfloat16 [256, 8, 2048], P('group', None, 'tensor')
The draws below stay inside these ranges and needn't reach their ends.
Inputs may be any that keep to these rules, and one draw needn't show every extreme that they name: source[h] is h or h - 1 modulo 8. For each page index k, the values decode_owner[h, k] over all h are all different; no row names one group more than 4 times, and some row names a group exactly 4 times.
All inputs are finite; a program needn't handle non-finite values.
Results may differ from the reference program's by a relative error of at most 0.012.
Values may be sent and summed in bfloat16 or wider, within the bound.
A program may use at most 192 MiB of HBM per device.

```python
import math
import jax
import jax.numpy as jnp
from jax import lax

D = 4096
HQ = 32
KVH = 8
HD = 128
PAGE = 8
BLOCK = 256
PREFIX = 8192
GROUPS = 8
NPAGE = 32
PREF_PAGES = 1024
KV_COLS = 2048
N_TENSOR = 4


def draw_prefix_pool(key, part):
    values = jax.random.normal(key, (GROUPS * 2 * PREF_PAGES, PAGE, KV_COLS), jnp.float32)
    values = jnp.clip(values, -5.0, 5.0)
    return values.astype(jnp.bfloat16)


def draw_source(key, part):
    indices = jnp.arange(GROUPS)
    coins = jax.random.randint(jax.random.fold_in(key, 2), (GROUPS,), 0, 2)
    middle = GROUPS // 2
    forced = (indices == 0) | (indices == middle)
    takes = jnp.logical_or(forced, coins == 1)
    picked = jnp.where(takes, indices - 1, indices)
    return (picked % GROUPS).astype(jnp.int32)


def draw_decode_owner(key, part):
    spread_count = min(GROUPS, NPAGE - NPAGE // 4)
    offsets_all = jax.random.permutation(jax.random.fold_in(key, 1), GROUPS)
    relabel = jax.random.permutation(jax.random.fold_in(key, 2), GROUPS)
    offsets = offsets_all[jnp.arange(NPAGE) % spread_count]
    indices = jnp.arange(GROUPS)
    return relabel[(indices[:, None] + offsets[None, :]) % GROUPS].astype(jnp.int32)


def touch_ends(result, rng, low, high):
    shape = result.shape
    place = [jax.random.randint(jax.random.fold_in(rng, axis), (), 0, shape[axis]) for axis in range(len(shape))]
    result = result.at[tuple(place)].set(low)
    longest = shape.index(max(shape))
    place[longest] = (place[longest] + 1) % shape[longest]
    return result.at[tuple(place)].set(high)


def block_levels(rng, dims, pieces, least, top_value):
    def one(position, shards_of):
        heights = jax.random.uniform(jax.random.fold_in(jax.random.fold_in(rng, 6), position), (shards_of,), jnp.float32, least / len(pieces), top_value / len(pieces))
        return jnp.repeat(jnp.exp(heights), dims[position] // shards_of).reshape((-1,) + (1,) * (len(dims) - position - 1))

    factor_of = one(*pieces[0])
    for cut in pieces[1:]:
        factor_of = factor_of * one(*cut)
    return factor_of


def scatter_about(key, extent, width, most, pieces=(), held_as=jnp.bfloat16):
    drawn = jax.random.normal(key, extent, jnp.float32) * width
    if len(pieces) > 0:
        drawn = block_levels(key, extent, pieces, -0.22, 0.18) * drawn
    return jnp.clip(drawn, min=-most, max=most).astype(held_as)


def setup_inputs(seed: int = 0) -> dict:
    arg_keys = jax.random.split(jax.random.key(seed), 12)
    hidden = scatter_about(arg_keys[0], (GROUPS, 2, BLOCK, D), 1.0, 6.0, ((0, 8), (2, 4)))
    norm_gain = jnp.clip(1.0 + 0.1 * jax.random.normal(arg_keys[1], (D,), jnp.float32), 0.5, 1.5).astype(jnp.bfloat16)
    w_query = scatter_about(arg_keys[2], (D, HQ * HD), D ** -0.5, 0.09375, ((1, 4),))
    w_key = scatter_about(arg_keys[3], (D, KVH * HD), D ** -0.5, 0.09375, ((1, 4),))
    w_value = scatter_about(arg_keys[4], (D, KVH * HD), D ** -0.5, 0.09375, ((1, 4),))
    w_output = scatter_about(arg_keys[5], (HQ * HD, D), (HQ * HD) ** -0.5, 0.09375, ((0, 4),))
    prefix_pool = draw_prefix_pool(jax.random.fold_in(arg_keys[11], 71), 0)
    page_table = jax.vmap(lambda own: jax.random.permutation(own, PREF_PAGES))(jax.random.split(arg_keys[7], GROUPS * 2)).reshape((GROUPS, 2, PREF_PAGES)).astype(jnp.int32)
    prefix_len = touch_ends(jax.random.randint(arg_keys[8], (GROUPS, 2), PREFIX // 8, PREFIX + 1), jax.random.fold_in(arg_keys[8], 1), PREFIX // 8, PREFIX).astype(jnp.int32)
    source = draw_source(jax.random.fold_in(arg_keys[11], 71), 0)
    decode_owner = draw_decode_owner(jax.random.fold_in(arg_keys[11], 71), 0)
    return {"hidden": hidden, "norm_gain": norm_gain, "w_query": w_query, "w_key": w_key, "w_value": w_value, "w_output": w_output, "prefix_pool": prefix_pool, "page_table": page_table, "prefix_len": prefix_len, "source": source, "decode_owner": decode_owner}


EPS = 1e-05
THETA = 500000.0

def rotate(values, positions):
    half_dim = values.shape[-1] // 2
    frequency = THETA ** (-(jnp.arange(half_dim, dtype=jnp.float32) * 2.0) / values.shape[-1])
    angles = positions[..., None] * frequency
    cosine = jnp.cos(angles)[..., None, :]
    sines = jnp.sin(angles)[..., None, :]
    first_half = values[..., :half_dim]
    second = values[..., half_dim:]
    return jnp.concatenate([first_half * cosine - second * sines, second * cosine + first_half * sines], axis=-1)

def reference(hidden, norm_gain, w_query, w_key, w_value, w_output, prefix_pool, page_table, prefix_len, source, decode_owner):
    group_size = HQ // KVH
    score_scale = 1.0 / math.sqrt(HD)
    flat_hidden = hidden.reshape(GROUPS * 2, BLOCK, D)
    flat_table = page_table.reshape(GROUPS * 2, PREF_PAGES)
    flat_len = prefix_len.reshape(GROUPS * 2)

    def one_group(slot_index):
        owner_group = source[slot_index].astype(jnp.int32)
        slot = jnp.where(owner_group == slot_index, 0, 1).astype(jnp.int32)
        entry = (owner_group * 2 + slot).astype(jnp.int32)
        prefix_count = flat_len[entry]
        block_rows = lax.dynamic_slice_in_dim(flat_hidden, entry, 1, 0)[0]
        block_f32 = block_rows.astype(jnp.float32)
        mean_square = lax.optimization_barrier(jnp.mean(block_f32 * block_f32, axis=-1, keepdims=True))
        normed = (block_f32 * lax.rsqrt(mean_square + EPS) * norm_gain.astype(jnp.float32)).astype(jnp.bfloat16)
        queries = jnp.dot(normed, w_query, preferred_element_type=jnp.float32).reshape(BLOCK, HQ, HD)
        new_keys = jnp.dot(normed, w_key, preferred_element_type=jnp.float32).reshape(BLOCK, KVH, HD)
        new_values = jnp.dot(normed, w_value, preferred_element_type=jnp.float32).reshape(BLOCK, KVH, HD).astype(jnp.bfloat16)
        positions = (prefix_count + jnp.arange(BLOCK, dtype=jnp.int32)).astype(jnp.float32)
        queries = rotate(queries, positions).astype(jnp.bfloat16)
        new_keys = rotate(new_keys, positions).astype(jnp.bfloat16)
        slot_order = lax.dynamic_slice_in_dim(flat_table, entry, 1, 0)[0].astype(jnp.int32)
        prefix_kv = jnp.take(prefix_pool, entry * PREF_PAGES + slot_order, axis=0)
        prefix_kv = prefix_kv.reshape(PREFIX, KVH, 2, HD)
        all_keys = jnp.concatenate([prefix_kv[:, :, 0], new_keys], axis=0)
        values = jnp.concatenate([prefix_kv[:, :, 1], new_values], axis=0)
        column = jnp.arange(PREFIX + BLOCK, dtype=jnp.int32)[None, :]
        row_index = jnp.arange(BLOCK, dtype=jnp.int32)[:, None]
        allowed = jnp.where(column < PREFIX, column < prefix_count, column - PREFIX <= row_index)
        grouped = queries.reshape(BLOCK, KVH, group_size, HD).astype(jnp.float32)
        scores = jnp.einsum('qhgd,khd->hgqk', grouped, all_keys.astype(jnp.float32)) * score_scale
        scores = jnp.where(allowed, scores, -jnp.inf)
        row_max = lax.optimization_barrier(jnp.max(scores, axis=-1, keepdims=True))
        exp_scores = jnp.where(allowed, jnp.exp(scores - row_max), 0.0)
        row_total = lax.optimization_barrier(jnp.sum(exp_scores, axis=-1))
        weights = exp_scores.astype(jnp.bfloat16)
        mixed_heads = jnp.einsum('hgqk,khd->qhgd', weights.astype(jnp.float32), values.astype(jnp.float32))
        attended = (mixed_heads / jnp.transpose(row_total, (2, 0, 1))[..., None]).astype(jnp.bfloat16)
        blocks = attended.reshape(BLOCK, N_TENSOR, HQ * HD // N_TENSOR).astype(jnp.float32)
        projections = w_output.reshape(N_TENSOR, HQ * HD // N_TENSOR, D).astype(jnp.float32)
        partial_value = jnp.einsum('qtc,tcd->tqd', blocks, projections).astype(jnp.bfloat16)
        summed = lax.optimization_barrier(jnp.sum(partial_value.astype(jnp.float32), axis=0))
        out_rows = (block_f32 + summed).astype(jnp.bfloat16)
        new_kv = jnp.stack([new_keys, new_values], axis=2).reshape(BLOCK, KV_COLS)
        return (out_rows, new_kv)
    block_outs, block_kv = lax.map(one_group, jnp.arange(GROUPS, dtype=jnp.int32))
    layer_out = block_outs.reshape(GROUPS * BLOCK, D)
    page_rows = block_kv.reshape(GROUPS * NPAGE, PAGE, KV_COLS)
    pool_slots = (decode_owner.astype(jnp.int32) * NPAGE + jnp.arange(NPAGE, dtype=jnp.int32)[None, :]).reshape(-1)
    kv_pool = jnp.zeros((GROUPS * NPAGE, PAGE, KV_COLS), jnp.bfloat16).at[pool_slots].set(page_rows)
    return (layer_out, kv_pool)
```

```python
import functools
import math

import jax
import jax.numpy as jnp
from jax import lax
from jax.experimental import pallas as pl
from jax.experimental.pallas import tpu as pltpu
from jax.sharding import PartitionSpec as P

HD = 128
PAGE = 8
EPS = 1e-05
THETA = 500000.0
CHUNK = 512
EXP_SCALE = math.log2(math.e) / math.sqrt(HD)


def shift(block, axis, distance):
    size = lax.axis_size(axis)
    return lax.ppermute(block, axis, [(i, (i + distance) % size) for i in range(size)])


def rope_tables(positions):
    half_dim = HD // 2
    frequency = THETA ** (-(jnp.arange(half_dim, dtype=jnp.float32) * 2.0) / HD)
    angles = positions[:, None] * frequency
    return jnp.cos(angles)[:, None, :], jnp.sin(angles)[:, None, :]


def rotate(values, tables):
    cosine, sines = tables
    half_dim = HD // 2
    first = values[..., :half_dim]
    second = values[..., half_dim:]
    return jnp.concatenate(
        [first * cosine - second * sines, second * cosine + first * sines], axis=-1
    )


def attention_kernel(base, kv_heads, with_new, *refs):
    if with_new:
        n_ref, table_ref, q_ref, new_ref, pool_ref, out_ref, m_ref, l_ref, buf, sems = refs
        acc_ref = out_ref
    else:
        n_ref, table_ref, q_ref, pool_ref, out_ref, m_ref, l_ref, acc_ref, buf, sems = refs
    count = n_ref[0]
    chunk = buf.shape[1]
    pages = chunk // PAGE
    last = table_ref.shape[0] // pages - 1
    columns = q_ref.shape[2]
    block = new_ref.shape[0] if with_new else 256

    def start(index, slot):
        for i in range(pages):
            page = table_ref[index * pages + i] + base
            pltpu.make_async_copy(
                pool_ref.at[page], buf.at[slot, pl.ds(i * PAGE, PAGE)], sems.at[slot]
            ).start()

    def wait(slot):
        pltpu.make_async_copy(buf.at[slot], buf.at[slot], sems.at[slot]).wait()

    def absorb(load, mask_of):
        for g in range(kv_heads):
            keys = load(g * 2 * HD)
            values_t = load(g * 2 * HD + HD).T
            for c in range(0, columns, block):
                span = slice(c, c + block)
                scores = jnp.dot(keys, q_ref[g, :, span], preferred_element_type=jnp.float32)
                if mask_of is not None:
                    scores = jnp.where(mask_of(scores.shape), scores, -jnp.inf)
                old = m_ref[g : g + 1, span]
                top = jnp.maximum(old, jnp.max(scores, axis=0, keepdims=True))
                fade = jnp.exp2((old - top) * EXP_SCALE)
                weights = jnp.exp2((scores - top) * EXP_SCALE)
                m_ref[g : g + 1, span] = top
                l_ref[g : g + 1, span] = l_ref[g : g + 1, span] * fade + jnp.sum(
                    weights, axis=0, keepdims=True
                )
                acc_ref[g, :, span] = acc_ref[g, :, span] * fade + jnp.dot(
                    values_t, weights.astype(jnp.bfloat16), preferred_element_type=jnp.float32
                )

    start(0, 0)
    m_ref[...] = jnp.full_like(m_ref, -jnp.inf)
    l_ref[...] = jnp.zeros_like(l_ref)
    acc_ref[...] = jnp.zeros_like(acc_ref)
    if with_new:
        absorb(
            lambda c: new_ref[:, c : c + HD],
            lambda shape: lax.broadcasted_iota(jnp.int32, shape, 0)
            <= lax.broadcasted_iota(jnp.int32, shape, 1),
        )
    full = count // chunk

    def step(index, carry):
        slot = index % 2
        wait(slot)
        start(jnp.minimum(index + 1, last), 1 - slot)
        absorb(lambda c: buf[slot, :, c : c + HD], None)
        return carry

    lax.fori_loop(0, full, step, 0)
    slot = full % 2
    wait(slot)

    @pl.when(count > full * chunk)
    def _():
        absorb(
            lambda c: buf[slot, :, c : c + HD],
            lambda shape: lax.broadcasted_iota(jnp.int32, shape, 0) + full * chunk < count,
        )

    if not with_new:
        total = l_ref[...]
        inverse = jnp.where(total > 0.0, 1.0 / jnp.where(total > 0.0, total, 1.0), 0.0)
        for g in range(kv_heads):
            out_ref[g] = (acc_ref[g] * inverse[g : g + 1]).astype(out_ref.dtype)


def attention(count, table, q_t, pool, base, new_kv=None):
    kv_heads, _, columns = q_t.shape
    with_new = new_kv is not None
    vmem = pl.BlockSpec(memory_space=pltpu.VMEM)
    smem = pl.BlockSpec(memory_space=pltpu.SMEM)
    scratch = [
        pltpu.VMEM((2, CHUNK, pool.shape[2]), jnp.bfloat16),
        pltpu.SemaphoreType.DMA((2,)),
    ]
    if not with_new:
        scratch = [pltpu.VMEM(q_t.shape, jnp.float32)] + scratch
    keys = table.shape[0] * PAGE
    stat = jax.ShapeDtypeStruct((kv_heads, columns), jnp.float32)
    return pl.pallas_call(
        functools.partial(attention_kernel, base, kv_heads, with_new),
        out_shape=(
            jax.ShapeDtypeStruct(q_t.shape, jnp.float32 if with_new else jnp.bfloat16),
            stat,
            stat,
        ),
        in_specs=[smem, smem, vmem]
        + ([vmem] if with_new else [])
        + [pl.BlockSpec(memory_space=pl.ANY)],
        out_specs=(vmem, vmem, vmem),
        scratch_shapes=scratch,
        cost_estimate=pl.CostEstimate(
            flops=2 * keys * kv_heads * columns * HD,
            transcendentals=keys * kv_heads * columns // 2,
            bytes_accessed=keys * pool.shape[2],
        ),
        name="own_attention" if with_new else "lent_attention",
    )(count.reshape(1), table, q_t, *([new_kv] if with_new else []), pool)


def local(
    hidden,
    norm_gain,
    w_query,
    w_key,
    w_value,
    w_output,
    prefix_pool,
    page_table,
    prefix_len,
    source,
    decode_owner,
):
    groups = lax.axis_size("group")
    tensors = lax.axis_size("tensor")
    my_group = lax.axis_index("group")
    query_width = w_query.shape[1]
    key_width = w_key.shape[1]
    query_heads = query_width // HD
    kv_heads = key_width // HD
    group_size = query_heads // kv_heads
    kv_cols = prefix_pool.shape[2]
    region = prefix_pool.shape[0] // 2
    lower_group = (my_group + groups - 1) % groups
    upper_group = (my_group + 1) % groups
    take_lower = source[my_group] == lower_group
    lend_upper = source[upper_group] == my_group
    own_len = prefix_len[my_group]
    prefix_count = jnp.where(take_lower, prefix_len[lower_group, 1], own_len[0])
    own_count = jnp.where(take_lower, 0, own_len[0])
    lent_count = jnp.where(lend_upper, own_len[1], 0)

    handed = shift(hidden[0, 1], "group", 1)
    rows = jnp.where(take_lower, handed, hidden[0, 0])
    rows_f32 = rows.astype(jnp.float32)
    mean_square = jnp.mean(rows_f32 * rows_f32, axis=-1, keepdims=True)
    normed = (rows_f32 * lax.rsqrt(mean_square + EPS) * norm_gain.astype(jnp.float32)).astype(
        jnp.bfloat16
    )
    flat = lax.all_gather(normed, "tensor", axis=0, tiled=True)
    block_len = flat.shape[0]
    positions = (prefix_count + jnp.arange(block_len, dtype=jnp.int32)).astype(jnp.float32)
    tables = rope_tables(positions)
    queries = rotate(
        jnp.dot(flat, w_query, preferred_element_type=jnp.float32).reshape(
            block_len, query_heads, HD
        ),
        tables,
    ).astype(jnp.bfloat16)
    q_t = jnp.transpose(
        queries.reshape(block_len, kv_heads, group_size, HD), (1, 3, 2, 0)
    ).reshape(kv_heads, HD, group_size * block_len)
    lent_q = shift(q_t, "group", -1)
    new_keys = rotate(
        jnp.dot(flat, w_key, preferred_element_type=jnp.float32).reshape(block_len, kv_heads, HD),
        tables,
    ).astype(jnp.bfloat16)
    new_values = (
        jnp.dot(flat, w_value, preferred_element_type=jnp.float32)
        .astype(jnp.bfloat16)
        .reshape(block_len, kv_heads, HD)
    )
    new_kv = jnp.stack([new_keys, new_values], axis=2).reshape(block_len, kv_cols)

    own_acc, own_max, own_sum = attention(
        own_count, page_table[0, 0], q_t, prefix_pool, 0, new_kv
    )
    lent_out, lent_max, lent_sum = attention(
        lent_count, page_table[0, 1], lent_q, prefix_pool, region
    )
    part, part_max, part_sum = shift((lent_out, lent_max, lent_sum), "group", 1)
    top = jnp.maximum(own_max, part_max)
    own_scale = jnp.exp2((own_max - top) * EXP_SCALE)
    part_scale = jnp.exp2((part_max - top) * EXP_SCALE) * part_sum
    total = own_sum * own_scale + part_scale
    attended = (
        (own_acc * own_scale[:, None] + part.astype(jnp.float32) * part_scale[:, None])
        / total[:, None]
    ).astype(jnp.bfloat16)
    attended = jnp.transpose(
        attended.reshape(kv_heads, HD, group_size, block_len), (3, 0, 2, 1)
    ).reshape(block_len, query_width)
    branch = lax.psum_scatter(
        jnp.dot(attended, w_output, preferred_element_type=jnp.float32).astype(jnp.bfloat16),
        "tensor",
        scatter_dimension=0,
        tiled=True,
    ).astype(jnp.float32)
    layer_out = (rows_f32 + branch).astype(jnp.bfloat16)

    page_count = block_len // PAGE
    spread_count = min(groups, page_count - page_count // 4)
    slot_cap = (page_count + spread_count - 1) // spread_count
    page_ids = jnp.arange(page_count)
    earlier = page_ids[None, :] < page_ids[:, None]
    same_dest = decode_owner[:, :, None] == decode_owner[:, None, :]
    page_ranks = jnp.sum(jnp.logical_and(same_dest, earlier[None]), axis=-1)
    my_dest = decode_owner[my_group]
    my_rank = page_ranks[my_group]
    slot_ids = jnp.arange(groups * slot_cap)
    send_select = jnp.logical_and(
        my_dest[None, :] == (slot_ids // slot_cap)[:, None],
        my_rank[None, :] == (slot_ids % slot_cap)[:, None],
    ).astype(jnp.bfloat16)
    paged = new_kv.reshape(page_count, PAGE * kv_cols)
    outgoing = (
        jnp.dot(send_select, paged, preferred_element_type=jnp.float32)
        .astype(jnp.bfloat16)
        .reshape(groups, slot_cap * PAGE * kv_cols)
    )
    incoming = lax.all_to_all(outgoing, "group", split_axis=0, concat_axis=0, tiled=True)
    recv_select = jnp.logical_and(
        (decode_owner.T == my_group)[:, :, None],
        page_ranks.T[:, :, None] == jnp.arange(slot_cap)[None, None, :],
    )
    recv_select = recv_select.reshape(page_count, groups * slot_cap).astype(jnp.bfloat16)
    kv_pool = jnp.dot(
        recv_select,
        incoming.reshape(groups * slot_cap, PAGE * kv_cols),
        preferred_element_type=jnp.float32,
    )
    kv_pool = kv_pool.astype(jnp.bfloat16).reshape(page_count, PAGE, kv_cols)
    return (layer_out, kv_pool)


def solution(mesh):
    return jax.shard_map(
        local,
        mesh=mesh,
        in_specs=(
            P("group", None, "tensor", None),
            P(),
            P(None, "tensor"),
            P(None, "tensor"),
            P(None, "tensor"),
            P("tensor", None),
            P("group", None, "tensor"),
            P("group", None, None),
            P(),
            P(),
            P(),
        ),
        out_specs=(P(("group", "tensor"), None), P("group", None, "tensor")),
        check_vma=False,
    )
```

```python
import functools
import math

import jax
import jax.numpy as jnp
from jax import lax
from jax.experimental import pallas as pl
from jax.experimental.pallas import tpu as pltpu
from jax.sharding import PartitionSpec as P

HD = 128
PAGE = 8
EPS = 1e-05
THETA = 500000.0
CHUNK = 1024
EXP_SCALE = math.log2(math.e) / math.sqrt(HD)


def shift(block, axis, distance):
    size = lax.axis_size(axis)
    return lax.ppermute(block, axis, [(i, (i + distance) % size) for i in range(size)])


def rope_tables(positions):
    half_dim = HD // 2
    frequency = THETA ** (-(jnp.arange(half_dim, dtype=jnp.float32) * 2.0) / HD)
    angles = positions[:, None] * frequency
    return jnp.cos(angles)[:, None, :], jnp.sin(angles)[:, None, :]


def rotate(values, tables):
    cosine, sines = tables
    half_dim = HD // 2
    first = values[..., :half_dim]
    second = values[..., half_dim:]
    return jnp.concatenate(
        [first * cosine - second * sines, second * cosine + first * sines], axis=-1
    )


def attention_kernel(base, kv_heads, with_new, *refs):
    if with_new:
        n_ref, table_ref, q_ref, new_ref, pool_ref, out_ref, m_ref, l_ref, buf, sems = refs
        acc_ref = out_ref
    else:
        n_ref, table_ref, q_ref, pool_ref, out_ref, m_ref, l_ref, acc_ref, buf, sems = refs
    count = n_ref[0]
    chunk = buf.shape[1]
    pages = chunk // PAGE
    last = table_ref.shape[0] // pages - 1
    columns = q_ref.shape[2]
    block = new_ref.shape[0] if with_new else 256

    def start(index, slot):
        for i in range(pages):
            page = table_ref[index * pages + i] + base
            pltpu.make_async_copy(
                pool_ref.at[page], buf.at[slot, pl.ds(i * PAGE, PAGE)], sems.at[slot]
            ).start()

    def wait(slot):
        pltpu.make_async_copy(buf.at[slot], buf.at[slot], sems.at[slot]).wait()

    def absorb(load, mask_of):
        def settle(g, span, fade, weights):
            acc_ref[g, :, span] = acc_ref[g, :, span] * fade + lax.dot_general(
                load(g * 2 * HD + HD),
                weights,
                (((0,), (0,)), ((), ())),
                preferred_element_type=jnp.float32,
            )

        tasks = [(g, slice(c, c + block)) for g in range(kv_heads) for c in range(0, columns, block)]

        def score(task):
            g, span = task
            return jnp.dot(
                load(g * 2 * HD), q_ref[g, :, span], preferred_element_type=jnp.float32
            )

        ahead = score(tasks[0])
        pending = None
        for i, (g, span) in enumerate(tasks):
            scores = ahead
            if i + 1 < len(tasks):
                ahead = score(tasks[i + 1])
            if mask_of is not None:
                scores = jnp.where(mask_of(scores.shape), scores, -jnp.inf)
            old = m_ref[g : g + 1, span]
            top = jnp.maximum(old, jnp.max(scores, axis=0, keepdims=True))
            fade = jnp.exp2((old - top) * EXP_SCALE)
            weights = jnp.exp2((scores - top) * EXP_SCALE)
            m_ref[g : g + 1, span] = top
            l_ref[g : g + 1, span] = l_ref[g : g + 1, span] * fade + jnp.sum(
                weights, axis=0, keepdims=True
            )
            weights = weights.astype(jnp.bfloat16)
            if pending is not None:
                settle(*pending)
            pending = (g, span, fade, weights)
        settle(*pending)

    start(0, 0)
    m_ref[...] = jnp.full_like(m_ref, -jnp.inf)
    l_ref[...] = jnp.zeros_like(l_ref)
    acc_ref[...] = jnp.zeros_like(acc_ref)
    if with_new:
        absorb(
            lambda c: new_ref[:, c : c + HD],
            lambda shape: lax.broadcasted_iota(jnp.int32, shape, 0)
            <= lax.broadcasted_iota(jnp.int32, shape, 1),
        )
    full = count // chunk

    def step(index, carry):
        slot = index % 2
        wait(slot)
        start(jnp.minimum(index + 1, last), 1 - slot)
        absorb(lambda c: buf[slot, :, c : c + HD], None)
        return carry

    lax.fori_loop(0, full, step, 0)
    slot = full % 2
    wait(slot)

    @pl.when(count > full * chunk)
    def _():
        absorb(
            lambda c: buf[slot, :, c : c + HD],
            lambda shape: lax.broadcasted_iota(jnp.int32, shape, 0) + full * chunk < count,
        )

    if not with_new:
        total = l_ref[...]
        inverse = jnp.where(total > 0.0, 1.0 / jnp.where(total > 0.0, total, 1.0), 0.0)
        for g in range(kv_heads):
            out_ref[g] = (acc_ref[g] * inverse[g : g + 1]).astype(out_ref.dtype)


def attention(count, table, q_t, pool, base, new_kv=None):
    kv_heads, _, columns = q_t.shape
    with_new = new_kv is not None
    vmem = pl.BlockSpec(memory_space=pltpu.VMEM)
    smem = pl.BlockSpec(memory_space=pltpu.SMEM)
    scratch = [
        pltpu.VMEM((2, CHUNK, pool.shape[2]), jnp.bfloat16),
        pltpu.SemaphoreType.DMA((2,)),
    ]
    if not with_new:
        scratch = [pltpu.VMEM(q_t.shape, jnp.float32)] + scratch
    keys = table.shape[0] * PAGE
    stat = jax.ShapeDtypeStruct((kv_heads, columns), jnp.float32)
    return pl.pallas_call(
        functools.partial(attention_kernel, base, kv_heads, with_new),
        out_shape=(
            jax.ShapeDtypeStruct(q_t.shape, jnp.float32 if with_new else jnp.bfloat16),
            stat,
            stat,
        ),
        in_specs=[smem, smem, vmem]
        + ([vmem] if with_new else [])
        + [pl.BlockSpec(memory_space=pl.ANY)],
        out_specs=(vmem, vmem, vmem),
        scratch_shapes=scratch,
        cost_estimate=pl.CostEstimate(
            flops=2 * keys * kv_heads * columns * HD,
            transcendentals=keys * kv_heads * columns // 2,
            bytes_accessed=keys * pool.shape[2],
        ),
        name="own_attention" if with_new else "lent_attention",
    )(count.reshape(1), table, q_t, *([new_kv] if with_new else []), pool)


MESH = pl.DeviceIdType.MESH


def gather_kernel(take_ref, hidden_ref, gain_ref, rows_ref, flat_ref, handed, hand_sems, ready, send, recv):
    group, groups = lax.axis_index("group"), lax.axis_size("group")
    me, size = lax.axis_index("tensor"), lax.axis_size("tensor")
    upper, lower = (group + 1) % groups, (group + groups - 1) % groups
    right, left = (me + 1) % size, (me + size - 1) % size
    barrier = pltpu.get_barrier_semaphore()
    for axis, other in (("group", upper), ("group", lower), ("tensor", right), ("tensor", left)):
        pl.semaphore_signal(barrier, inc=1, device_id={axis: other}, device_id_type=MESH)
    pl.semaphore_wait(barrier, 4)
    hand = pltpu.make_async_remote_copy(
        src_ref=hidden_ref.at[1],
        dst_ref=handed,
        send_sem=hand_sems.at[0],
        recv_sem=hand_sems.at[1],
        device_id={"group": upper},
        device_id_type=MESH,
    )
    hand.start()
    hand.wait()
    count, width = handed.shape
    take = take_ref[0] > 0
    tile = 16
    for r in range(0, count, tile):
        span = slice(r, r + tile)
        rows = jnp.where(take, handed[span, :].astype(jnp.float32), hidden_ref[0, span, :].astype(jnp.float32))
        rows_ref[span, :] = rows.astype(rows_ref.dtype)
        mean_square = jnp.mean(rows * rows, axis=-1, keepdims=True)
        flat_ref[pl.ds(pl.multiple_of(me * count + r, tile), tile), :] = (
            rows * lax.rsqrt(mean_square + EPS) * gain_ref[...].astype(jnp.float32)
        ).astype(flat_ref.dtype)
    for other in (right, left):
        pl.semaphore_signal(ready, inc=1, device_id={"tensor": other}, device_id_type=MESH)
    pl.semaphore_wait(ready, 2)

    half = count // 2
    reach = size // 2

    def piece(direction, distance, part):
        source = (me - direction * (distance - 1) + size) % size
        ref = flat_ref.at[pl.ds(pl.multiple_of(source * count + part * half, half), half)]
        lane = 0 if direction > 0 else 1
        slot = (distance - 1) * 2 + part
        return pltpu.make_async_remote_copy(
            src_ref=ref,
            dst_ref=ref,
            send_sem=send.at[lane, slot],
            recv_sem=recv.at[lane, slot],
            device_id={"tensor": right if direction > 0 else left},
            device_id_type=MESH,
        )

    sent = []
    for distance in range(1, reach + 1):
        for order in range(2):
            for direction in (1, -1):
                part = order if direction > 0 else 1 - order
                if distance == reach and order == 1 and size % 2 == 0:
                    continue
                if distance > 1:
                    piece(direction, distance - 1, part).wait_recv()
                copy = piece(direction, distance, part)
                copy.start()
                sent.append((direction, distance, part))
    relayed = {(d, k - 1, p) for d, k, p in sent if k > 1}
    for direction, distance, part in sent:
        copy = piece(direction, distance, part)
        copy.wait_send()
        if (direction, distance, part) not in relayed:
            copy.wait_recv()


def gather_rows(take, hidden, gain, tensors):
    _, count, width = hidden.shape
    vmem = pl.BlockSpec(memory_space=pltpu.VMEM)
    pieces = max(2, tensors // 2 * 2)
    return pl.pallas_call(
        gather_kernel,
        out_shape=(
            jax.ShapeDtypeStruct((count, width), hidden.dtype),
            jax.ShapeDtypeStruct((count * tensors, width), hidden.dtype),
        ),
        in_specs=[pl.BlockSpec(memory_space=pltpu.SMEM), vmem, vmem],
        out_specs=(vmem, vmem),
        scratch_shapes=[
            pltpu.VMEM((count, width), hidden.dtype),
            pltpu.SemaphoreType.DMA((2,)),
            pltpu.SemaphoreType.REGULAR,
            pltpu.SemaphoreType.DMA((2, pieces)),
            pltpu.SemaphoreType.DMA((2, pieces)),
        ],
        compiler_params=pltpu.CompilerParams(collective_id=0, has_side_effects=True),
        name="gather_rows",
    )(take.astype(jnp.int32).reshape(1), hidden, gain.reshape(1, -1))


def exchange_kernel(
    give_ref, keep_ref, pages_ref, q_ref, lent_ref, pool_ref, staged, landed, q_sems, own_sem, send, recv
):
    me, groups = lax.axis_index("group"), lax.axis_size("group")
    cap = staged.shape[1]

    def stage(index, carry):
        staged[index // cap, index % cap] = pages_ref[give_ref[index]]
        return carry

    lax.fori_loop(0, groups * cap, stage, 0)
    barrier = pltpu.get_barrier_semaphore()
    for k in range(1, groups):
        pl.semaphore_signal(barrier, inc=1, device_id={"group": (me + k) % groups}, device_id_type=MESH)
    pl.semaphore_wait(barrier, groups - 1)
    lend = pltpu.make_async_remote_copy(
        src_ref=q_ref,
        dst_ref=lent_ref,
        send_sem=q_sems.at[0],
        recv_sem=q_sems.at[1],
        device_id={"group": (me + groups - 1) % groups},
        device_id_type=MESH,
    )
    lend.start()
    own = pltpu.make_async_copy(staged.at[me], landed.at[me], own_sem)
    own.start()
    copies = []
    for k in range(1, groups):
        peer = (me + k) % groups
        copy = pltpu.make_async_remote_copy(
            src_ref=staged.at[peer],
            dst_ref=landed.at[me],
            send_sem=send.at[k],
            recv_sem=recv.at[k],
            device_id={"group": peer},
            device_id_type=MESH,
        )
        copy.start()
        copies.append(copy)
    own.wait()
    for copy in copies:
        copy.wait()

    def store(index, carry):
        place = keep_ref[index]
        pool_ref[index] = landed[place // cap, place % cap]
        return carry

    lax.fori_loop(0, pages_ref.shape[0], store, 0)
    lend.wait()


def exchange(give, keep, pages, q_t, groups, cap):
    vmem = pl.BlockSpec(memory_space=pltpu.VMEM)
    smem = pl.BlockSpec(memory_space=pltpu.SMEM)
    box = pltpu.VMEM((groups, cap) + pages.shape[1:], pages.dtype)
    return pl.pallas_call(
        exchange_kernel,
        out_shape=(
            jax.ShapeDtypeStruct(q_t.shape, q_t.dtype),
            jax.ShapeDtypeStruct(pages.shape, pages.dtype),
        ),
        in_specs=[smem, smem, vmem, vmem],
        out_specs=(vmem, vmem),
        scratch_shapes=[
            box,
            box,
            pltpu.SemaphoreType.DMA((2,)),
            pltpu.SemaphoreType.DMA,
            pltpu.SemaphoreType.DMA((groups,)),
            pltpu.SemaphoreType.DMA((groups,)),
        ],
        compiler_params=pltpu.CompilerParams(collective_id=1, has_side_effects=True),
        name="exchange",
    )(give, keep, pages, q_t)


def local(
    hidden,
    norm_gain,
    w_query,
    w_key,
    w_value,
    w_output,
    prefix_pool,
    page_table,
    prefix_len,
    source,
    decode_owner,
):
    groups = lax.axis_size("group")
    tensors = lax.axis_size("tensor")
    my_group = lax.axis_index("group")
    query_width = w_query.shape[1]
    key_width = w_key.shape[1]
    query_heads = query_width // HD
    kv_heads = key_width // HD
    group_size = query_heads // kv_heads
    kv_cols = prefix_pool.shape[2]
    region = prefix_pool.shape[0] // 2
    lower_group = (my_group + groups - 1) % groups
    upper_group = (my_group + 1) % groups
    take_lower = source[my_group] == lower_group
    lend_upper = source[upper_group] == my_group
    own_len = prefix_len[my_group]
    prefix_count = jnp.where(take_lower, prefix_len[lower_group, 1], own_len[0])
    own_count = jnp.where(take_lower, 0, own_len[0])
    lent_count = jnp.where(lend_upper, own_len[1], 0)

    rows, flat = gather_rows(take_lower, hidden[0], norm_gain, tensors)
    block_len = flat.shape[0]
    positions = (prefix_count + jnp.arange(block_len, dtype=jnp.int32)).astype(jnp.float32)
    tables = rope_tables(positions)
    queries = rotate(
        jnp.dot(flat, w_query, preferred_element_type=jnp.float32).reshape(
            block_len, query_heads, HD
        ),
        tables,
    ).astype(jnp.bfloat16)
    q_t = jnp.transpose(
        queries.reshape(block_len, kv_heads, group_size, HD), (1, 3, 2, 0)
    ).reshape(kv_heads, HD, group_size * block_len)
    new_keys = rotate(
        jnp.dot(flat, w_key, preferred_element_type=jnp.float32).reshape(block_len, kv_heads, HD),
        tables,
    ).astype(jnp.bfloat16)
    new_values = (
        jnp.dot(flat, w_value, preferred_element_type=jnp.float32)
        .astype(jnp.bfloat16)
        .reshape(block_len, kv_heads, HD)
    )
    new_kv = jnp.stack([new_keys, new_values], axis=2).reshape(block_len, kv_cols)

    page_count = block_len // PAGE
    spread_count = min(groups, page_count - page_count // 4)
    slot_cap = (page_count + spread_count - 1) // spread_count
    page_ids = jnp.arange(page_count)
    earlier = page_ids[None, :] < page_ids[:, None]
    same_dest = decode_owner[:, :, None] == decode_owner[:, None, :]
    page_ranks = jnp.sum(jnp.logical_and(same_dest, earlier[None]), axis=-1, dtype=jnp.int32)
    box_slots = decode_owner * slot_cap + page_ranks
    give = jnp.sum(
        jnp.where(
            box_slots[my_group][None, :] == jnp.arange(groups * slot_cap)[:, None],
            page_ids[None, :],
            0,
        ),
        axis=1,
        dtype=jnp.int32,
    )
    keep = jnp.sum(
        jnp.where(
            decode_owner == my_group, jnp.arange(groups)[:, None] * slot_cap + page_ranks, 0
        ),
        axis=0,
        dtype=jnp.int32,
    )
    lent_q, kv_pool = exchange(
        give, keep, new_kv.reshape(page_count, PAGE, kv_cols), q_t, groups, slot_cap
    )

    own_acc, own_max, own_sum = attention(
        own_count, page_table[0, 0], q_t, prefix_pool, 0, new_kv
    )
    lent_out, lent_max, lent_sum = attention(
        lent_count, page_table[0, 1], lent_q, prefix_pool, region
    )
    part, part_stats = shift((lent_out, jnp.stack([lent_max, lent_sum])), "group", 1)
    part_max, part_sum = part_stats[0], part_stats[1]
    top = jnp.maximum(own_max, part_max)
    own_scale = jnp.exp2((own_max - top) * EXP_SCALE)
    part_scale = jnp.exp2((part_max - top) * EXP_SCALE) * part_sum
    total = own_sum * own_scale + part_scale
    attended = (
        (own_acc * own_scale[:, None] + part.astype(jnp.float32) * part_scale[:, None])
        / total[:, None]
    ).astype(jnp.bfloat16)
    attended = jnp.transpose(
        attended.reshape(kv_heads, HD, group_size, block_len), (3, 0, 2, 1)
    ).reshape(block_len, query_width)
    branch = lax.psum_scatter(
        jnp.dot(attended, w_output, preferred_element_type=jnp.float32).astype(jnp.bfloat16),
        "tensor",
        scatter_dimension=0,
        tiled=True,
    ).astype(jnp.float32)
    layer_out = (rows.astype(jnp.float32) + branch).astype(jnp.bfloat16)
    return (layer_out, kv_pool)


def solution(mesh):
    return jax.shard_map(
        local,
        mesh=mesh,
        in_specs=(
            P("group", None, "tensor", None),
            P(),
            P(None, "tensor"),
            P(None, "tensor"),
            P(None, "tensor"),
            P("tensor", None),
            P("group", None, "tensor"),
            P("group", None, None),
            P(),
            P(),
            P(),
        ),
        out_specs=(P(("group", "tensor"), None), P("group", None, "tensor")),
        check_vma=False,
    )
```

```python
import functools
import math

import jax
import jax.numpy as jnp
from jax import lax
from jax.experimental import pallas as pl
from jax.experimental.pallas import tpu as pltpu
from jax.sharding import PartitionSpec as P

HD = 128
PAGE = 8
EPS = 1e-05
THETA = 500000.0
CHUNK = 1024
EXP_SCALE = math.log2(math.e) / math.sqrt(HD)


def shift(block, axis, distance):
    size = lax.axis_size(axis)
    return lax.ppermute(block, axis, [(i, (i + distance) % size) for i in range(size)])


def rope_tables(positions):
    half_dim = HD // 2
    frequency = THETA ** (-(jnp.arange(half_dim, dtype=jnp.float32) * 2.0) / HD)
    angles = positions[:, None] * frequency
    return jnp.cos(angles)[:, None, :], jnp.sin(angles)[:, None, :]


def rotate(values, tables):
    cosine, sines = tables
    half_dim = HD // 2
    first = values[..., :half_dim]
    second = values[..., half_dim:]
    return jnp.concatenate(
        [first * cosine - second * sines, second * cosine + first * sines], axis=-1
    )


def attention_kernel(base, kv_heads, with_new, *refs):
    if with_new:
        n_ref, table_ref, q_ref, new_ref, pool_ref, out_ref, m_ref, l_ref, buf, sems = refs
        acc_ref = out_ref
    else:
        n_ref, table_ref, q_ref, pool_ref, out_ref, m_ref, l_ref, acc_ref, buf, sems = refs
    count = n_ref[0]
    chunk = buf.shape[1]
    pages = chunk // PAGE
    last = table_ref.shape[0] // pages - 1
    columns = q_ref.shape[2]
    block = new_ref.shape[0] if with_new else 256

    def start(index, slot):
        for i in range(pages):
            page = table_ref[index * pages + i] + base
            pltpu.make_async_copy(
                pool_ref.at[page], buf.at[slot, pl.ds(i * PAGE, PAGE)], sems.at[slot]
            ).start()

    def wait(slot):
        pltpu.make_async_copy(buf.at[slot], buf.at[slot], sems.at[slot]).wait()

    def absorb(load, mask_of):
        def settle(g, span, fade, weights):
            acc_ref[g, :, span] = acc_ref[g, :, span] * fade + lax.dot_general(
                load(g * 2 * HD + HD),
                weights,
                (((0,), (0,)), ((), ())),
                preferred_element_type=jnp.float32,
            )

        tasks = [(g, slice(c, c + block)) for g in range(kv_heads) for c in range(0, columns, block)]

        def score(task):
            g, span = task
            return jnp.dot(
                load(g * 2 * HD), q_ref[g, :, span], preferred_element_type=jnp.float32
            )

        ahead = score(tasks[0])
        pending = None
        for i, (g, span) in enumerate(tasks):
            scores = ahead
            if i + 1 < len(tasks):
                ahead = score(tasks[i + 1])
            if mask_of is not None:
                scores = jnp.where(mask_of(scores.shape), scores, -jnp.inf)
            old = m_ref[g : g + 1, span]
            top = jnp.maximum(old, jnp.max(scores, axis=0, keepdims=True))
            fade = jnp.exp2((old - top) * EXP_SCALE)
            weights = jnp.exp2((scores - top) * EXP_SCALE)
            m_ref[g : g + 1, span] = top
            l_ref[g : g + 1, span] = l_ref[g : g + 1, span] * fade + jnp.sum(
                weights, axis=0, keepdims=True
            )
            weights = weights.astype(jnp.bfloat16)
            if pending is not None:
                settle(*pending)
            pending = (g, span, fade, weights)
        settle(*pending)

    start(0, 0)
    m_ref[...] = jnp.full_like(m_ref, -jnp.inf)
    l_ref[...] = jnp.zeros_like(l_ref)
    acc_ref[...] = jnp.zeros_like(acc_ref)
    if with_new:
        absorb(
            lambda c: new_ref[:, c : c + HD],
            lambda shape: lax.broadcasted_iota(jnp.int32, shape, 0)
            <= lax.broadcasted_iota(jnp.int32, shape, 1),
        )
    full = count // chunk

    def step(index, carry):
        slot = index % 2
        wait(slot)
        start(jnp.minimum(index + 1, last), 1 - slot)
        absorb(lambda c: buf[slot, :, c : c + HD], None)
        return carry

    lax.fori_loop(0, full, step, 0)
    slot = full % 2
    wait(slot)

    @pl.when(count > full * chunk)
    def _():
        absorb(
            lambda c: buf[slot, :, c : c + HD],
            lambda shape: lax.broadcasted_iota(jnp.int32, shape, 0) + full * chunk < count,
        )

    if not with_new:
        total = l_ref[...]
        inverse = jnp.where(total > 0.0, 1.0 / jnp.where(total > 0.0, total, 1.0), 0.0)
        for g in range(kv_heads):
            out_ref[g] = (acc_ref[g] * inverse[g : g + 1]).astype(out_ref.dtype)


def attention(count, table, q_t, pool, base, new_kv=None):
    kv_heads, _, columns = q_t.shape
    with_new = new_kv is not None
    vmem = pl.BlockSpec(memory_space=pltpu.VMEM)
    smem = pl.BlockSpec(memory_space=pltpu.SMEM)
    scratch = [
        pltpu.VMEM((2, CHUNK, pool.shape[2]), jnp.bfloat16),
        pltpu.SemaphoreType.DMA((2,)),
    ]
    if not with_new:
        scratch = [pltpu.VMEM(q_t.shape, jnp.float32)] + scratch
    keys = table.shape[0] * PAGE
    stat = jax.ShapeDtypeStruct((kv_heads, columns), jnp.float32)
    return pl.pallas_call(
        functools.partial(attention_kernel, base, kv_heads, with_new),
        out_shape=(
            jax.ShapeDtypeStruct(q_t.shape, jnp.float32 if with_new else jnp.bfloat16),
            stat,
            stat,
        ),
        in_specs=[smem, smem, vmem]
        + ([vmem] if with_new else [])
        + [pl.BlockSpec(memory_space=pl.ANY)],
        out_specs=(vmem, vmem, vmem),
        scratch_shapes=scratch,
        cost_estimate=pl.CostEstimate(
            flops=2 * keys * kv_heads * columns * HD,
            transcendentals=keys * kv_heads * columns // 2,
            bytes_accessed=keys * pool.shape[2],
        ),
        name="own_attention" if with_new else "lent_attention",
    )(count.reshape(1), table, q_t, *([new_kv] if with_new else []), pool)


MESH = pl.DeviceIdType.MESH


def greet(semaphore, me, size, others=0):
    for direction in (1, -1):
        target = me + direction

        @pl.when(jnp.logical_and(target >= 0, target < size))
        def _():
            pl.semaphore_signal(
                semaphore,
                inc=1,
                device_id={"tensor": jnp.clip(target, 0, size - 1)},
                device_id_type=MESH,
            )

    peers = jnp.where(me > 0, 1, 0) + jnp.where(me < size - 1, 1, 0)
    pl.semaphore_wait(semaphore, peers + others)


def project_kernel(mixed_ref, w_hbm, rows_ref, out_ref, weights, sums, inbox, w_sems, send, recv):
    me, size = lax.axis_index("tensor"), lax.axis_size("tensor")
    count, width = rows_ref.shape
    tiles = weights.shape[0]
    wide = weights.shape[2]

    def fetch(i):
        return pltpu.make_async_copy(
            w_hbm.at[:, pl.ds(pl.multiple_of(i * wide, wide), wide)], weights.at[i], w_sems.at[i]
        )

    for i in range(tiles):
        fetch(i).start()
    greet(pltpu.get_barrier_semaphore(), me, size)

    def hop(direction, chunk):
        lane = 0 if direction > 0 else 1
        return pltpu.make_async_remote_copy(
            src_ref=sums.at[chunk],
            dst_ref=inbox.at[lane, chunk],
            send_sem=send.at[chunk],
            recv_sem=recv.at[lane, chunk],
            device_id={"tensor": jnp.clip(me + direction, 0, size - 1)},
            device_id_type=MESH,
        )

    order = []
    for k in range((size + 1) // 2):
        order += [size - 1 - k] + ([k] if k != size - 1 - k else [])
    for place, chunk in enumerate(order):

        def product(i, carry, first=place == 0, chunk=chunk):
            if first:
                fetch(i).wait()
            sums[chunk, :, pl.ds(pl.multiple_of(i * wide, wide), wide)] = jnp.dot(
                mixed_ref[chunk * count : (chunk + 1) * count, :],
                weights[i],
                preferred_element_type=jnp.float32,
            ).astype(sums.dtype)
            return carry

        lax.fori_loop(0, tiles, product, 0)
        if chunk > 0:

            @pl.when(me == 0)
            def _(chunk=chunk):
                hop(1, chunk).start()

        if chunk < size - 1:

            @pl.when(me == size - 1)
            def _(chunk=chunk):
                hop(-1, chunk).start()

    def relay(direction, chunk):
        lane = 0 if direction > 0 else 1
        hop(direction, chunk).wait_recv()

        def add(i, carry):
            span = pl.ds(pl.multiple_of(i * wide, wide), wide)
            sums[chunk, :, span] = (
                sums[chunk, :, span].astype(jnp.float32)
                + inbox[lane, chunk, :, span].astype(jnp.float32)
            ).astype(sums.dtype)
            return carry

        lax.fori_loop(0, tiles, add, 0)
        hop(direction, chunk).start()

    def up(chunk):
        @pl.when(jnp.logical_and(me > 0, me < chunk))
        def _():
            relay(1, chunk)

    def down(chunk):
        @pl.when(jnp.logical_and(me < size - 1, me > chunk))
        def _():
            relay(-1, chunk)

    @pl.when(me < size // 2)
    def _():
        for k in range(size):
            up(size - 1 - k)
            down(k)

    @pl.when(me >= size // 2)
    def _():
        for k in range(size):
            down(k)
            up(size - 1 - k)

    @pl.when(me > 0)
    def _():
        hop(1, me).wait_recv()

    @pl.when(me == 0)
    def _():
        inbox[0, me] = jnp.zeros(inbox.shape[2:], inbox.dtype)

    @pl.when(me < size - 1)
    def _():
        hop(-1, me).wait_recv()

    @pl.when(me == size - 1)
    def _():
        inbox[1, me] = jnp.zeros(inbox.shape[2:], inbox.dtype)

    def finish(i, carry):
        span = pl.ds(pl.multiple_of(i * wide, wide), wide)
        branch = sums[me, :, span].astype(jnp.float32) + (
            inbox[0, me, :, span].astype(jnp.float32) + inbox[1, me, :, span].astype(jnp.float32)
        )
        out_ref[:, span] = (rows_ref[:, span].astype(jnp.float32) + branch).astype(out_ref.dtype)
        return carry

    lax.fori_loop(0, tiles, finish, 0)
    for chunk in range(size):

        @pl.when(me < chunk)
        def _(chunk=chunk):
            hop(1, chunk).wait_send()

        @pl.when(me > chunk)
        def _(chunk=chunk):
            hop(-1, chunk).wait_send()


def project(mixed, weights, rows, tensors):
    count, width = rows.shape
    wide = 512 if width % 512 == 0 else width
    tiles = width // wide
    vmem = pl.BlockSpec(memory_space=pltpu.VMEM)
    return pl.pallas_call(
        project_kernel,
        out_shape=jax.ShapeDtypeStruct((count, width), rows.dtype),
        in_specs=[vmem, pl.BlockSpec(memory_space=pl.ANY), vmem],
        out_specs=vmem,
        scratch_shapes=[
            pltpu.VMEM((tiles, weights.shape[0], wide), weights.dtype),
            pltpu.VMEM((tensors, count, width), rows.dtype),
            pltpu.VMEM((2, tensors, count, width), rows.dtype),
            pltpu.SemaphoreType.DMA((tiles,)),
            pltpu.SemaphoreType.DMA((tensors,)),
            pltpu.SemaphoreType.DMA((2, tensors)),
        ],
        compiler_params=pltpu.CompilerParams(collective_id=2, has_side_effects=True),
        name="project",
    )(mixed, weights, rows)


def gather_kernel(take_ref, hidden_ref, gain_ref, rows_ref, flat_ref, handed, hand_sems, ready, send, recv):
    group, groups = lax.axis_index("group"), lax.axis_size("group")
    me, size = lax.axis_index("tensor"), lax.axis_size("tensor")
    upper, lower = (group + 1) % groups, (group + groups - 1) % groups
    barrier = pltpu.get_barrier_semaphore()
    for other in (upper, lower):
        pl.semaphore_signal(barrier, inc=1, device_id={"group": other}, device_id_type=MESH)
    greet(barrier, me, size, 2)
    hand = pltpu.make_async_remote_copy(
        src_ref=hidden_ref.at[1],
        dst_ref=handed,
        send_sem=hand_sems.at[0],
        recv_sem=hand_sems.at[1],
        device_id={"group": upper},
        device_id_type=MESH,
    )
    hand.start()
    hand.wait()
    count, width = handed.shape
    take = take_ref[0] > 0
    tile = 16
    for r in range(0, count, tile):
        span = slice(r, r + tile)
        rows = jnp.where(take, handed[span, :].astype(jnp.float32), hidden_ref[0, span, :].astype(jnp.float32))
        rows_ref[span, :] = rows.astype(rows_ref.dtype)
        mean_square = jnp.mean(rows * rows, axis=-1, keepdims=True)
        flat_ref[pl.ds(pl.multiple_of(me * count + r, tile), tile), :] = (
            rows * lax.rsqrt(mean_square + EPS) * gain_ref[...].astype(jnp.float32)
        ).astype(flat_ref.dtype)
    greet(ready, me, size)

    def piece(direction, source, step):
        ref = flat_ref.at[pl.ds(pl.multiple_of(source * count, count), count)]
        lane = 0 if direction > 0 else 1
        return pltpu.make_async_remote_copy(
            src_ref=ref,
            dst_ref=ref,
            send_sem=send.at[lane, step],
            recv_sem=recv.at[lane, step],
            device_id={"tensor": jnp.clip(me + direction, 0, size - 1)},
            device_id_type=MESH,
        )

    for step in range(size):
        for direction in (1, -1):
            source = me - direction * step
            valid = jnp.logical_and(source >= 0, source < size)
            target = me + direction
            sends = jnp.logical_and(valid, jnp.logical_and(target >= 0, target < size))
            if step > 0:

                @pl.when(valid)
                def _():
                    piece(direction, source, step - 1).wait_recv()

            if step < size - 1:

                @pl.when(sends)
                def _():
                    piece(direction, source, step).start()

    for step in range(size - 1):
        for direction in (1, -1):
            source = me - direction * step
            valid = jnp.logical_and(source >= 0, source < size)
            target = me + direction
            sends = jnp.logical_and(valid, jnp.logical_and(target >= 0, target < size))

            @pl.when(sends)
            def _():
                piece(direction, source, step).wait_send()


def gather_rows(take, hidden, gain, tensors):
    _, count, width = hidden.shape
    vmem = pl.BlockSpec(memory_space=pltpu.VMEM)
    return pl.pallas_call(
        gather_kernel,
        out_shape=(
            jax.ShapeDtypeStruct((count, width), hidden.dtype),
            jax.ShapeDtypeStruct((count * tensors, width), hidden.dtype),
        ),
        in_specs=[pl.BlockSpec(memory_space=pltpu.SMEM), vmem, vmem],
        out_specs=(vmem, vmem),
        scratch_shapes=[
            pltpu.VMEM((count, width), hidden.dtype),
            pltpu.SemaphoreType.DMA((2,)),
            pltpu.SemaphoreType.REGULAR,
            pltpu.SemaphoreType.DMA((2, tensors)),
            pltpu.SemaphoreType.DMA((2, tensors)),
        ],
        compiler_params=pltpu.CompilerParams(collective_id=0, has_side_effects=True),
        name="gather_rows",
    )(take.astype(jnp.int32).reshape(1), hidden, gain.reshape(1, -1))


def exchange_kernel(
    give_ref, keep_ref, pages_ref, q_ref, lent_ref, pool_ref, staged, landed, q_sems, own_sem, send, recv
):
    me, groups = lax.axis_index("group"), lax.axis_size("group")
    cap = staged.shape[1]

    def stage(index, carry):
        staged[index // cap, index % cap] = pages_ref[give_ref[index]]
        return carry

    lax.fori_loop(0, groups * cap, stage, 0)
    barrier = pltpu.get_barrier_semaphore()
    for k in range(1, groups):
        pl.semaphore_signal(barrier, inc=1, device_id={"group": (me + k) % groups}, device_id_type=MESH)
    pl.semaphore_wait(barrier, groups - 1)
    lend = pltpu.make_async_remote_copy(
        src_ref=q_ref,
        dst_ref=lent_ref,
        send_sem=q_sems.at[0],
        recv_sem=q_sems.at[1],
        device_id={"group": (me + groups - 1) % groups},
        device_id_type=MESH,
    )
    lend.start()
    own = pltpu.make_async_copy(staged.at[me], landed.at[me], own_sem)
    own.start()
    copies = []
    for k in range(1, groups):
        peer = (me + k) % groups
        copy = pltpu.make_async_remote_copy(
            src_ref=staged.at[peer],
            dst_ref=landed.at[me],
            send_sem=send.at[k],
            recv_sem=recv.at[k],
            device_id={"group": peer},
            device_id_type=MESH,
        )
        copy.start()
        copies.append(copy)
    own.wait()
    for copy in copies:
        copy.wait()

    def store(index, carry):
        place = keep_ref[index]
        pool_ref[index] = landed[place // cap, place % cap]
        return carry

    lax.fori_loop(0, pages_ref.shape[0], store, 0)
    lend.wait()


def exchange(give, keep, pages, q_t, groups, cap):
    vmem = pl.BlockSpec(memory_space=pltpu.VMEM)
    smem = pl.BlockSpec(memory_space=pltpu.SMEM)
    box = pltpu.VMEM((groups, cap) + pages.shape[1:], pages.dtype)
    return pl.pallas_call(
        exchange_kernel,
        out_shape=(
            jax.ShapeDtypeStruct(q_t.shape, q_t.dtype),
            jax.ShapeDtypeStruct(pages.shape, pages.dtype),
        ),
        in_specs=[smem, smem, vmem, vmem],
        out_specs=(vmem, vmem),
        scratch_shapes=[
            box,
            box,
            pltpu.SemaphoreType.DMA((2,)),
            pltpu.SemaphoreType.DMA,
            pltpu.SemaphoreType.DMA((groups,)),
            pltpu.SemaphoreType.DMA((groups,)),
        ],
        compiler_params=pltpu.CompilerParams(collective_id=1, has_side_effects=True),
        name="exchange",
    )(give, keep, pages, q_t)


def local(
    hidden,
    norm_gain,
    w_query,
    w_key,
    w_value,
    w_output,
    prefix_pool,
    page_table,
    prefix_len,
    source,
    decode_owner,
):
    groups = lax.axis_size("group")
    tensors = lax.axis_size("tensor")
    my_group = lax.axis_index("group")
    query_width = w_query.shape[1]
    key_width = w_key.shape[1]
    query_heads = query_width // HD
    kv_heads = key_width // HD
    group_size = query_heads // kv_heads
    kv_cols = prefix_pool.shape[2]
    region = prefix_pool.shape[0] // 2
    lower_group = (my_group + groups - 1) % groups
    upper_group = (my_group + 1) % groups
    take_lower = source[my_group] == lower_group
    lend_upper = source[upper_group] == my_group
    own_len = prefix_len[my_group]
    prefix_count = jnp.where(take_lower, prefix_len[lower_group, 1], own_len[0])
    own_count = jnp.where(take_lower, 0, own_len[0])
    lent_count = jnp.where(lend_upper, own_len[1], 0)

    rows, flat = gather_rows(take_lower, hidden[0], norm_gain, tensors)
    block_len = flat.shape[0]
    positions = (prefix_count + jnp.arange(block_len, dtype=jnp.int32)).astype(jnp.float32)
    tables = rope_tables(positions)
    queries = rotate(
        jnp.dot(flat, w_query, preferred_element_type=jnp.float32).reshape(
            block_len, query_heads, HD
        ),
        tables,
    ).astype(jnp.bfloat16)
    q_t = jnp.transpose(
        queries.reshape(block_len, kv_heads, group_size, HD), (1, 3, 2, 0)
    ).reshape(kv_heads, HD, group_size * block_len)
    new_keys = rotate(
        jnp.dot(flat, w_key, preferred_element_type=jnp.float32).reshape(block_len, kv_heads, HD),
        tables,
    ).astype(jnp.bfloat16)
    new_values = (
        jnp.dot(flat, w_value, preferred_element_type=jnp.float32)
        .astype(jnp.bfloat16)
        .reshape(block_len, kv_heads, HD)
    )
    new_kv = jnp.stack([new_keys, new_values], axis=2).reshape(block_len, kv_cols)

    page_count = block_len // PAGE
    spread_count = min(groups, page_count - page_count // 4)
    slot_cap = (page_count + spread_count - 1) // spread_count
    page_ids = jnp.arange(page_count)
    earlier = page_ids[None, :] < page_ids[:, None]
    same_dest = decode_owner[:, :, None] == decode_owner[:, None, :]
    page_ranks = jnp.sum(jnp.logical_and(same_dest, earlier[None]), axis=-1, dtype=jnp.int32)
    box_slots = decode_owner * slot_cap + page_ranks
    give = jnp.sum(
        jnp.where(
            box_slots[my_group][None, :] == jnp.arange(groups * slot_cap)[:, None],
            page_ids[None, :],
            0,
        ),
        axis=1,
        dtype=jnp.int32,
    )
    keep = jnp.sum(
        jnp.where(
            decode_owner == my_group, jnp.arange(groups)[:, None] * slot_cap + page_ranks, 0
        ),
        axis=0,
        dtype=jnp.int32,
    )
    lent_q, kv_pool = exchange(
        give, keep, new_kv.reshape(page_count, PAGE, kv_cols), q_t, groups, slot_cap
    )

    own_acc, own_max, own_sum = attention(
        own_count, page_table[0, 0], q_t, prefix_pool, 0, new_kv
    )
    lent_out, lent_max, lent_sum = attention(
        lent_count, page_table[0, 1], lent_q, prefix_pool, region
    )
    part, part_stats = shift((lent_out, jnp.stack([lent_max, lent_sum])), "group", 1)
    part_max, part_sum = part_stats[0], part_stats[1]
    top = jnp.maximum(own_max, part_max)
    own_scale = jnp.exp2((own_max - top) * EXP_SCALE)
    part_scale = jnp.exp2((part_max - top) * EXP_SCALE) * part_sum
    total = own_sum * own_scale + part_scale
    attended = (
        (own_acc * own_scale[:, None] + part.astype(jnp.float32) * part_scale[:, None])
        / total[:, None]
    ).astype(jnp.bfloat16)
    attended = jnp.transpose(
        attended.reshape(kv_heads, HD, group_size, block_len), (3, 0, 2, 1)
    ).reshape(block_len, query_width)
    layer_out = project(attended, w_output, rows, tensors)
    return (layer_out, kv_pool)


def solution(mesh):
    return jax.shard_map(
        local,
        mesh=mesh,
        in_specs=(
            P("group", None, "tensor", None),
            P(),
            P(None, "tensor"),
            P(None, "tensor"),
            P(None, "tensor"),
            P("tensor", None),
            P("group", None, "tensor"),
            P("group", None, None),
            P(),
            P(),
            P(),
        ),
        out_specs=(P(("group", "tensor"), None), P("group", None, "tensor")),
        check_vma=False,
    )
```
